32 devices in a mesh: fsdp: 32 (over z, y, x, core).
Axes of the slice: x: 2, y: 2, z: 4, core: 2. Of those that a mesh axis runs over, the one named last changes fastest.
Arguments:
- tokens: bfloat16 [32768, 768], P('fsdp'), may hold values from -6 to 6
- depth_stack: bfloat16 [4, 32768, 768], P(None, 'fsdp'), may hold values from -12 to 12
- prefix: int32 [32], replicated, may hold values from 102 to 512, as said below
- ln1_gain: bfloat16 [768], P('fsdp'), may hold values from 0.5 to 1.5
- ln1_bias: bfloat16 [768], P('fsdp'), may hold values from -2 to 2
- w_qkv: bfloat16 [768, 2304], P('fsdp'), may hold values from -0.3125 to 0.3125
- w_out: bfloat16 [768, 768], P('fsdp'), may hold values from -0.875 to 0.875
- ln2_gain: bfloat16 [768], P('fsdp'), may hold values from 0.5 to 1.5
- ln2_bias: bfloat16 [768], P('fsdp'), may hold values from -2 to 2
- w_up: bfloat16 [768, 3072], P('fsdp'), may hold values from -0.21875 to 0.21875
- b_up: bfloat16 [3072], P('fsdp'), may hold values from -3 to 3
- w_down: bfloat16 [3072, 768], P('fsdp'), may hold values from -0.109375 to 0.109375
- b_down: bfloat16 [768], P('fsdp'), may hold values from -3 to 3
- dwa_weights: float32 [5], replicated, may hold values from 0.3 to 1.2
- cotangent: bfloat16 [32768, 768], P('fsdp'), may hold values from -6 to 6
Outputs:
- layer_out: bfloat16 [32768, 768], P('fsdp')
- grad_tokens: float32 [32768, 768], P('fsdp')
- grad_stack: float32 [4, 32768, 768], P(None, 'fsdp')
- grad_ln1_gain: float32 [768], P('fsdp')
- grad_ln1_bias: float32 [768], P('fsdp')
- grad_w_qkv: float32 [768, 2304], P('fsdp')
- grad_w_out: float32 [768, 768], P('fsdp')
- grad_ln2_gain: float32 [768], P('fsdp')
- grad_ln2_bias: float32 [768], P('fsdp')
- grad_w_up: float32 [768, 3072], P('fsdp')
- grad_b_up: float32 [3072], P('fsdp')
- grad_w_down: float32 [3072, 768], P('fsdp')
- grad_b_down: float32 [768], P('fsdp')
- grad_dwa: float32 [5], replicated
The draws below stay inside these ranges and needn't reach their ends.
Inputs may be any that keep to these rules, and one draw needn't show every extreme that they name: `prefix`: between a tenth and half of the sequence's length; some sequence reaches each end.
All inputs are finite; a program needn't handle non-finite values.
Results may differ from the reference program's by a relative error of at most 0.013.
Values may be sent and summed in bfloat16 or wider, within the bound.
No kernel may reach another device: no remote copies, remote signals or barrier semaphores. Data moves between devices by JAX's collectives and lax.ppermute only.
A program may use at most 192 MiB of HBM per device.

```python
import math
import jax
import jax.numpy as jnp
from jax import lax

D = 768
HEADS = 12
FF = 3072
SEQ = 1024
TOKENS = 32768
SEQS = 32


def draw_prefix(key, part):
    first_key, second_key = jax.random.split(key, 2)
    lowest = SEQ // 10
    highest = SEQ // 2
    values = jax.random.randint(first_key, (SEQS,), lowest, highest + 1)
    order = jax.random.permutation(second_key, SEQS)
    values = values.at[order[0]].set(highest)
    values = values.at[order[1]].set(lowest)
    return values.astype(jnp.int32)


def draw_depth_stack(key, part):
    rows_pos = jnp.arange(TOKENS).astype(jnp.float32)
    row_scale = 1.0 + 2.0 * rows_pos / TOKENS
    base = jnp.clip(jax.random.normal(key, (4, TOKENS, D), jnp.float32), -4.0, 4.0)
    values = base * row_scale[None, :, None]
    return values.astype(jnp.bfloat16)


def block_scale(rng, dims, shards, low, high):
    def one(dim, shards_of):
        draws = jax.random.uniform(jax.random.fold_in(jax.random.fold_in(rng, 6), dim), (shards_of,), jnp.float32, low / len(shards), high / len(shards))
        return jnp.repeat(jnp.exp(draws), dims[dim] // shards_of).reshape((-1,) + (1,) * (len(dims) - dim - 1))

    level = one(*shards[0])
    for cut in shards[1:]:
        level = level * one(*cut)
    return level


def normal_values(key, shape, scale, bound, cuts=(), dtype=jnp.bfloat16):
    values = jax.random.normal(key, shape, jnp.float32) * scale
    if len(cuts) > 0:
        values = block_scale(key, shape, cuts, -0.22, 0.18) * values
    return jnp.clip(values, min=-bound, max=bound).astype(dtype)


def setup_inputs(seed: int = 0) -> dict:
    key_list = jax.random.split(jax.random.key(seed), 16)
    tokens = normal_values(key_list[0], (TOKENS, D), 1.0, 6.0, ((0, 32),))
    depth_stack = draw_depth_stack(jax.random.fold_in(key_list[15], 71), 0)
    prefix = draw_prefix(jax.random.fold_in(key_list[15], 71), 0)
    ln1_gain = jnp.clip(1.0 + 0.1 * jax.random.normal(key_list[3], (D,), jnp.float32), 0.5, 1.5).astype(jnp.bfloat16)
    ln1_bias = normal_values(key_list[4], (D,), 0.3, 2.0, ((0, 32),))
    w_qkv = normal_values(key_list[5], (D, 3 * D), (D // 2) ** -0.5, 0.3125, ((0, 32),))
    w_out = normal_values(key_list[6], (D, D), (D // 16) ** -0.5, 0.875, ((0, 32),))
    ln2_gain = jnp.clip(1.0 + 0.1 * jax.random.normal(key_list[7], (D,), jnp.float32), 0.5, 1.5).astype(jnp.bfloat16)
    ln2_bias = normal_values(key_list[8], (D,), 0.3, 2.0, ((0, 32),))
    w_up = normal_values(key_list[9], (D, FF), D ** -0.5, 0.21875, ((0, 32),))
    b_up = normal_values(key_list[10], (FF,), 0.5, 3.0, ((0, 32),))
    w_down = normal_values(key_list[11], (FF, D), FF ** -0.5, 0.109375, ((0, 32),))
    b_down = normal_values(key_list[12], (D,), 0.5, 3.0, ((0, 32),))
    dwa_weights = jnp.clip(jax.random.uniform(key_list[13], (5,), jnp.float32, 0.3, 1.2), 0.3, 1.2)
    cotangent = normal_values(key_list[14], (TOKENS, D), 1.0, 6.0, ((0, 32),))
    return dict(tokens=tokens, depth_stack=depth_stack, prefix=prefix, ln1_gain=ln1_gain, ln1_bias=ln1_bias, w_qkv=w_qkv, w_out=w_out, ln2_gain=ln2_gain, ln2_bias=ln2_bias, w_up=w_up, b_up=b_up, w_down=w_down, b_down=b_down, dwa_weights=dwa_weights, cotangent=cotangent)


NORM_EPS = 1e-05
NEG_FILL = -1e+30
HIGHEST = lax.Precision.HIGHEST

@jax.custom_vjp
def low(v):
    return lax.optimization_barrier(v.astype(jnp.bfloat16)).astype(jnp.float32)

@jax.custom_vjp
def low_back(v):
    return v

def low_keep(v):
    return (low(v), None)

def low_pass(kept, grad):
    return (grad,)

def back_keep(v):
    return (v, None)

def back_low(kept, grad):
    return (low(grad),)
low.defvjp(low_keep, low_pass)
low_back.defvjp(back_keep, back_low)

def layer_norm(values, gain, shift):
    center = values - lax.optimization_barrier(jnp.mean(values, axis=-1, keepdims=True))
    spread = lax.optimization_barrier(jnp.mean(center * center, axis=-1, keepdims=True))
    return center * lax.rsqrt(spread + NORM_EPS) * gain + shift

def rotary_tables(positions, head_size):
    half_size = head_size // 2
    freqs = jnp.exp(jnp.arange(half_size).astype(jnp.float32) * (-2.0 * math.log(10000.0) / head_size))
    angles = positions[:, None] * freqs[None, :]
    cosine = jnp.cos(angles)
    sine = jnp.sin(angles)
    return (jnp.concatenate([cosine, cosine], axis=-1)[:, None, :], jnp.concatenate([sine, sine], axis=-1)[:, None, :])

def rotate(values, cosine, sine):
    half_size = values.shape[-1] // 2
    turned = jnp.concatenate([-values[..., half_size:], values[..., :half_size]], axis=-1)
    return values * cosine + turned * sine

def attend(pieces):
    queries, key_block, values, prefix_len = pieces
    seq_len = queries.shape[0]
    scores = low_back(jnp.einsum('qhe,khe->hqk', queries, key_block, precision=HIGHEST) * queries.shape[-1] ** (-0.5))
    query_pos = jnp.arange(seq_len)[:, None]
    key_pos = jnp.arange(seq_len)[None, :]
    allowed = (key_pos <= query_pos) | (key_pos < prefix_len)
    scores = jnp.where(allowed[None], scores, NEG_FILL)
    top_score = lax.optimization_barrier(jnp.max(scores, axis=-1, keepdims=True))
    raised = jnp.exp(scores - top_score)
    attn_probs = low(raised / lax.optimization_barrier(jnp.sum(raised, axis=-1, keepdims=True)))
    return jnp.einsum('hqk,khe->qhe', attn_probs, values, precision=HIGHEST)

def forward(tokens, depth_stack, ln1_gain, ln1_bias, w_qkv, w_out, ln2_gain, ln2_bias, w_up, b_up, w_down, b_down, dwa_weights, prefix):
    model_width = tokens.shape[1]
    head_size = model_width // HEADS
    cosine, sine = rotary_tables(jnp.arange(SEQ).astype(jnp.float32), head_size)
    normed = low(layer_norm(tokens, ln1_gain, ln1_bias))
    project = low_back(jnp.dot(normed, w_qkv, precision=HIGHEST))
    shaped = project.reshape(SEQS, SEQ, 3, HEADS, head_size)
    queries = low(rotate(shaped[:, :, 0], cosine, sine))
    key_block = low(rotate(shaped[:, :, 1], cosine, sine))
    values = low(shaped[:, :, 2])
    mixed = lax.map(jax.checkpoint(attend), (queries, key_block, values, prefix))
    heads_out = low(low_back(mixed.reshape(SEQS * SEQ, model_width)))
    resid = tokens + low_back(jnp.dot(heads_out, w_out, precision=HIGHEST))
    normed_two = low(layer_norm(resid, ln2_gain, ln2_bias))
    before = low_back(jnp.dot(normed_two, w_up, precision=HIGHEST) + b_up)
    hidden = low(jax.nn.gelu(before, approximate=True))
    block_out = resid + low_back(jnp.dot(hidden, w_down, precision=HIGHEST) + b_down)
    result = dwa_weights[4] * block_out
    for level in range(4):
        result = result + dwa_weights[level] * depth_stack[level]
    return result

def reference(tokens, depth_stack, prefix, ln1_gain, ln1_bias, w_qkv, w_out, ln2_gain, ln2_bias, w_up, b_up, w_down, b_down, dwa_weights, cotangent):
    floats = tuple((array_in.astype(jnp.float32) for array_in in (tokens, depth_stack, ln1_gain, ln1_bias, w_qkv, w_out, ln2_gain, ln2_bias, w_up, b_up, w_down, b_down, dwa_weights)))

    def wrapped(*inputs):
        return forward(*inputs, prefix)
    result, pullback = jax.vjp(wrapped, *floats)
    grads = pullback(cotangent.astype(jnp.float32))
    return (result.astype(jnp.bfloat16), grads[0], grads[1], grads[2], grads[3], grads[4], grads[5], grads[6], grads[7], grads[8], grads[9], grads[10], grads[11], grads[12])
```

```python
from functools import partial
import math

import jax
import jax.numpy as jnp
from jax import lax
from jax.experimental import pallas as pl
from jax.experimental.pallas import tpu as pltpu
from jax.sharding import PartitionSpec as P

HEADS = 12
NORM_EPS = 1e-05
NEG_FILL = -1e30
BF = jnp.bfloat16
F32 = jnp.float32
ROWS_Q = 256


def pairs_of(count, even_mask, odd_mask):
    return [(i, i ^ (odd_mask if i & 1 else even_mask)) for i in range(count)]


def send(value, count, even_mask, odd_mask=None):
    odd_mask = even_mask if odd_mask is None else odd_mask
    return lax.ppermute(value, "fsdp", pairs_of(count, even_mask, odd_mask))


def relative_places(count, me):
    owner = jnp.arange(count, dtype=jnp.int32)
    rel = owner ^ me
    x_bit = (rel >> 1) & 1
    y_bit = (rel >> 2) & 1
    odd = (owner & 1) == 1
    first = jnp.where(odd, y_bit, x_bit)
    second = jnp.where(odd, x_bit, y_bit)
    z_count = count // 8
    return (((rel & 1) * 2 + second) * 2 + first) * z_count + (rel >> 3)


def owners_in_order(count, me):
    place = jnp.arange(count, dtype=jnp.int32)
    z_count = count // 8
    core = place // (4 * z_count)
    second = (place // (2 * z_count)) & 1
    first = (place // z_count) & 1
    odd = ((me ^ core) & 1) == 1
    x_bit = jnp.where(odd, second, first)
    y_bit = jnp.where(odd, first, second)
    return ((place % z_count) * 8 + y_bit * 4 + x_bit * 2 + core) ^ me


def order_gathered(own, other, places):
    half, rows, cols = own.shape

    def body(places_ref, own_ref, other_ref, out_ref):
        place = places_ref[pl.program_id(0)]

        @pl.when(place < half)
        def _():
            out_ref[...] = own_ref[...]

        @pl.when(place >= half)
        def _():
            out_ref[...] = other_ref[...]

    block = (1, rows, cols)
    out = pl.pallas_call(
        body,
        out_shape=jax.ShapeDtypeStruct((2 * half, rows, cols), own.dtype),
        grid_spec=pltpu.PrefetchScalarGridSpec(
            num_scalar_prefetch=1,
            grid=(2 * half,),
            in_specs=[
                pl.BlockSpec(block, lambda t, p: (p[t] % half, 0, 0)),
                pl.BlockSpec(block, lambda t, p: (p[t] % half, 0, 0)),
            ],
            out_specs=pl.BlockSpec(block, lambda t, p: (t, 0, 0)),
        ),
        name="order_gathered",
    )(places, own, other)
    return out.reshape(2 * half * rows, cols)


def order_grads(parts, owners, count):
    rows = parts[0].shape[0] // count
    cols = [p.shape[1] for p in parts]
    total = sum(cols)
    quarter = count // 4
    views = [p.reshape(count, rows, p.shape[1]) for p in parts]
    n_parts = len(parts)

    def body(owners_ref, *refs):
        place = pl.program_id(0)
        for dest, lo, hi in zip(
            refs[n_parts:], (0, quarter, 2 * quarter), (quarter, 2 * quarter, count)
        ):

            @pl.when((place >= lo) & (place < hi))
            def _():
                at = 0
                for k in range(n_parts):
                    dest[:, :, at : at + cols[k]] = refs[k][...]
                    at += cols[k]

    def out_spec(lo, size):
        return pl.BlockSpec((1, rows, total), lambda t, o: (jnp.clip(t - lo, 0, size - 1), 0, 0))

    return pl.pallas_call(
        body,
        out_shape=(
            jax.ShapeDtypeStruct((quarter, rows, total), BF),
            jax.ShapeDtypeStruct((quarter, rows, total), BF),
            jax.ShapeDtypeStruct((2 * quarter, rows, total), BF),
        ),
        grid_spec=pltpu.PrefetchScalarGridSpec(
            num_scalar_prefetch=1,
            grid=(count,),
            in_specs=[pl.BlockSpec((1, rows, c), lambda t, o: (o[t], 0, 0)) for c in cols],
            out_specs=[
                out_spec(0, quarter),
                out_spec(quarter, quarter),
                out_spec(2 * quarter, 2 * quarter),
            ],
        ),
        name="order_grads",
    )(owners, *views)


def add_up(*terms):
    total = terms[0].astype(F32)
    for term in terms[1:]:
        total = total + term.astype(F32)
    return total


def fast_path(count, rows):
    return count >= 8 and count <= 64 and count & (count - 1) == 0 and rows % 8 == 0


def gather_blocks(shard, count):
    block = jnp.stack([shard] + [send(shard, count, 8 * k) for k in range(1, count // 8)])
    block = jnp.concatenate([block, send(block, count, 2, 4)])
    block = jnp.concatenate([block, send(block, count, 4, 2)])
    return block, send(block, count, 1)


def scatter_blocks(low, high, sent, count, wire):
    half = count // 4
    got = send(sent, count, 1)
    high = add_up(high, got[half:]).astype(wire)
    low = add_up(low, got[:half])
    got = send(high, count, 4, 2)
    half //= 2
    high = add_up(low[half:], got[half:]).astype(wire)
    low = add_up(low[:half], got[:half])
    low = add_up(low, send(high, count, 2, 4))
    rest = [send(low[k].astype(wire), count, 8 * k) for k in range(1, count // 8)]
    return add_up(low[0], *rest)


def gather_weight(shard, count, places):
    if not fast_path(count, shard.shape[0]):
        return lax.all_gather(shard, "fsdp", axis=0, tiled=True)
    return order_gathered(*gather_blocks(shard, count), places)


def scatter_grad(parts, count, owners):
    rows = parts[0].shape[0] // count
    if not fast_path(count, rows):
        whole = jnp.concatenate([p.astype(F32) for p in parts], axis=1)
        return lax.psum_scatter(whole, "fsdp", scatter_dimension=0, tiled=True)
    return scatter_blocks(*order_grads(parts, owners, count), count, BF)


def rope_tables(count_rows, head_size):
    half_size = head_size // 2
    freqs = jnp.exp(
        jnp.arange(half_size).astype(F32) * (-2.0 * math.log(10000.0) / head_size)
    )
    angles = jnp.arange(count_rows).astype(F32)[:, None] * freqs[None, :]
    cosine = jnp.cos(angles)
    sine = jnp.sin(angles)
    return jnp.concatenate([cosine] * 4, axis=-1), jnp.concatenate([-sine, sine] * 2, axis=-1)


def swap_halves(u):
    lane = lax.broadcasted_iota(jnp.int32, u.shape, 1)
    return jnp.where(lane % 64 < 32, pltpu.roll(u, 96, 1), pltpu.roll(u, 32, 1))


def project_body(x_ref, gain_ref, bias_ref, w_ref, cos_ref, sin_ref, out_ref, normed_ref):
    step = pl.program_id(0)

    @pl.when(step == 0)
    def _():
        x = x_ref[...].astype(F32)
        center = x - jnp.mean(x, axis=-1, keepdims=True)
        spread = jnp.mean(center * center, axis=-1, keepdims=True)
        normed_ref[...] = (
            center * lax.rsqrt(spread + NORM_EPS) * gain_ref[...] + bias_ref[...]
        ).astype(BF)

    y = jnp.dot(normed_ref[...], w_ref[...], preferred_element_type=F32)
    width = w_ref.shape[1]
    per_part = pl.num_programs(0) // 3

    @pl.when(step < 2 * per_part)
    def _():
        scale = jnp.where(step < per_part, 0.125, 1.0)
        for k in range(width // 128):
            u = y[:, k * 128 : (k + 1) * 128]
            turned = u * cos_ref[...] + swap_halves(u) * sin_ref[...]
            out_ref[:, k * 128 : (k + 1) * 128] = (turned.astype(BF) * scale.astype(BF)).astype(BF)

    @pl.when(step >= 2 * per_part)
    def _():
        out_ref[...] = y.astype(BF)


def project(x, gain, bias, w, cos, sin):
    rows, width = x.shape
    block = 256
    full = lambda shape: pl.BlockSpec(shape, lambda j: (0, 0))
    return pl.pallas_call(
        project_body,
        out_shape=(
            jax.ShapeDtypeStruct((rows, w.shape[1]), BF),
            jax.ShapeDtypeStruct((rows, width), BF),
        ),
        grid=(w.shape[1] // block,),
        in_specs=[
            full((rows, width)),
            full((1, width)),
            full((1, width)),
            pl.BlockSpec((width, block), lambda j: (0, j)),
            full((rows, 128)),
            full((rows, 128)),
        ],
        out_specs=(pl.BlockSpec((rows, block), lambda j: (0, j)), full((rows, width))),
        name="project",
    )(x, gain, bias, w, cos, sin)


def nt(a, b):
    return lax.dot_general(a, b, (((1,), (1,)), ((), ())), preferred_element_type=F32)


def tn(a, b):
    return lax.dot_general(a, b, (((0,), (0,)), ((), ())), preferred_element_type=F32)


def key_span(block_idx, rows):
    return max((block_idx + 1) * ROWS_Q, rows // 2)


def allowed_of(block_idx, span, prefix_len):
    query_pos = lax.broadcasted_iota(jnp.int32, (ROWS_Q, span), 0) + block_idx * ROWS_Q
    key_pos = lax.broadcasted_iota(jnp.int32, (ROWS_Q, span), 1)
    return key_pos <= jnp.maximum(query_pos, prefix_len - 1)


def attend_body(prefix_ref, q_ref, k_ref, v_ref, out_ref, lse_ref):
    rows = q_ref.shape[0]
    prefix_len = prefix_ref[0]
    for head in range(2):
        cols = slice(head * 64, head * 64 + 64)
        for b in range(rows // ROWS_Q):
            span = key_span(b, rows)
            here = slice(b * ROWS_Q, (b + 1) * ROWS_Q)
            scores = nt(q_ref[here, cols], k_ref[:span, cols])
            scores = jnp.where(allowed_of(b, span, prefix_len), scores, NEG_FILL)
            top = jnp.max(scores, axis=-1, keepdims=True)
            raised = jnp.exp(scores - top)
            total = jnp.sum(raised, axis=-1, keepdims=True)
            out = jnp.dot(raised.astype(BF), v_ref[:span, cols], preferred_element_type=F32)
            out_ref[here, cols] = (out / total).astype(BF)
            lse_ref[0, here, cols] = jnp.broadcast_to(top + jnp.log(total), (ROWS_Q, 64))


def attend(qkv, prefix_len):
    rows = qkv.shape[0]
    groups = qkv.shape[1] // 384
    part = lambda k: pl.BlockSpec((rows, 128), lambda j, p: (0, j + k * groups))
    return pl.pallas_call(
        attend_body,
        out_shape=(
            jax.ShapeDtypeStruct((rows, groups * 128), BF),
            jax.ShapeDtypeStruct((groups, rows, 128), F32),
        ),
        grid_spec=pltpu.PrefetchScalarGridSpec(
            num_scalar_prefetch=1,
            grid=(groups,),
            in_specs=[part(0), part(1), part(2)],
            out_specs=(
                pl.BlockSpec((rows, 128), lambda j, p: (0, j)),
                pl.BlockSpec((1, rows, 128), lambda j, p: (j, 0, 0)),
            ),
        ),
        name="attend",
    )(prefix_len, qkv, qkv, qkv)


def attend_back_body(
    prefix_ref, q_ref, k_ref, v_ref, g_ref, lse_ref, cos_ref, sin_ref,
    dq_ref, dk_ref, dv_ref, q_acc, k_acc, v_acc,
):
    rows = q_ref.shape[0]
    prefix_len = prefix_ref[0]
    for head in range(2):
        cols = slice(head * 64, head * 64 + 64)
        for b in reversed(range(rows // ROWS_Q)):
            span = key_span(b, rows)
            here = slice(b * ROWS_Q, (b + 1) * ROWS_Q)
            q = q_ref[here, cols]
            g = g_ref[here, cols]
            k = k_ref[:span, cols]
            scores = nt(q, k)
            lse = lse_ref[0, here, head * 64 : head * 64 + 1]
            probs = jnp.where(
                allowed_of(b, span, prefix_len), jnp.exp(jnp.minimum(scores - lse, 1.0)), 0.0
            )
            grad_probs = nt(g, v_ref[:span, cols])
            delta = jnp.sum(probs * grad_probs, axis=-1, keepdims=True)
            grad_scores = (probs * (grad_probs - delta)).astype(BF)
            q_acc[here, cols] = jnp.dot(grad_scores, k, preferred_element_type=F32) * 0.125
            grad_k = tn(grad_scores, q)
            grad_v = tn(probs.astype(BF), g)
            if span == rows and b == rows // ROWS_Q - 1:
                k_acc[:, cols] = grad_k
                v_acc[:, cols] = grad_v
            else:
                k_acc[:span, cols] += grad_k
                v_acc[:span, cols] += grad_v
    cos = cos_ref[...]
    sin = sin_ref[...]
    dq_ref[...] = (q_acc[...] * cos - swap_halves(q_acc[...]) * sin).astype(BF)
    dk_ref[...] = (k_acc[...] * cos - swap_halves(k_acc[...]) * sin).astype(BF)
    dv_ref[...] = v_acc[...].astype(BF)


def attend_back(qkv, grad_heads, lse, cos, sin, prefix_len):
    rows = qkv.shape[0]
    groups = qkv.shape[1] // 384
    part = lambda k: pl.BlockSpec((rows, 128), lambda j, p: (0, j + k * groups))
    full = pl.BlockSpec((rows, 128), lambda j, p: (0, 0))
    out = jax.ShapeDtypeStruct((rows, groups * 128), BF)
    return pl.pallas_call(
        attend_back_body,
        out_shape=(out, out, out),
        grid_spec=pltpu.PrefetchScalarGridSpec(
            num_scalar_prefetch=1,
            grid=(groups,),
            in_specs=[
                part(0),
                part(1),
                part(2),
                part(0),
                pl.BlockSpec((1, rows, 128), lambda j, p: (j, 0, 0)),
                full,
                full,
            ],
            out_specs=(part(0), part(0), part(0)),
            scratch_shapes=[pltpu.VMEM((rows, 128), F32)] * 3,
        ),
        name="attend_back",
    )(prefix_len, qkv, qkv, qkv, grad_heads, lse, cos, sin)


def layer_norm(values, gain, shift):
    center = values - jnp.mean(values, axis=-1, keepdims=True)
    spread = jnp.mean(center * center, axis=-1, keepdims=True)
    return center * lax.rsqrt(spread + NORM_EPS) * gain + shift


def gather_vectors(vectors, count, places):
    sizes = [v.shape[0] for v in vectors]
    packed = jnp.concatenate(vectors)
    if fast_path(count, 8):
        packed = jnp.pad(packed, (0, -packed.shape[0] % 128)).reshape(1, -1)
        everywhere = jnp.concatenate(gather_blocks(packed, count))[:, 0]
        everywhere = jnp.take(everywhere, places, axis=0)
    else:
        everywhere = lax.all_gather(packed, "fsdp", axis=0)
    out = []
    at = 0
    for size in sizes:
        out.append(everywhere[:, at : at + size].reshape(1, count * size).astype(F32))
        at += size
    return out


def scatter_vectors(vectors, count, owners):
    rows = [v.reshape(count, -1) for v in vectors]
    packed = jnp.concatenate(rows, axis=1)
    if fast_path(count, 8):
        packed = jnp.pad(packed, ((0, 0), (0, -packed.shape[1] % 128)))
        packed = jnp.take(packed, owners, axis=0)[:, None]
        quarter = count // 4
        owned = scatter_blocks(
            packed[:quarter], packed[quarter : 2 * quarter], packed[2 * quarter :], count, F32
        )[0]
    else:
        owned = lax.psum_scatter(packed, "fsdp", scatter_dimension=0, tiled=True)[0]
    out = []
    at = 0
    for row in rows:
        out.append(owned[at : at + row.shape[1]])
        at += row.shape[1]
    return out


def sum_everywhere(values, count):
    if not fast_path(count, 8):
        return jnp.sum(lax.all_gather(values, "fsdp", axis=0), axis=0)
    bit = 1
    while bit < count:
        values = values + send(values, count, bit)
        bit *= 2
    return values


def shards(
    count,
    tokens,
    depth_stack,
    prefix,
    ln1_gain,
    ln1_bias,
    w_qkv,
    w_out,
    ln2_gain,
    ln2_bias,
    w_up,
    b_up,
    w_down,
    b_down,
    dwa_weights,
    cotangent,
):
    me = lax.axis_index("fsdp")
    places = relative_places(count, me)
    owners = owners_in_order(count, me)
    gain_one, bias_one, gain_two, bias_two, bias_down, bias_up = gather_vectors(
        (ln1_gain, ln1_bias, ln2_gain, ln2_bias, b_down, b_up), count, places
    )
    proj_qkv = gather_weight(w_qkv, count, places)
    proj_out = gather_weight(w_out, count, places)
    proj_up = gather_weight(w_up, count, places)
    proj_down = gather_weight(w_down, count, places)

    count_rows, model_width = tokens.shape
    head_size = model_width // HEADS
    prefix_len = lax.dynamic_slice(prefix, (me,), (1,))
    cos, sin = rope_tables(count_rows, head_size)
    inputs_f = tokens.astype(F32)
    grad_out = cotangent.astype(F32)

    partial_dots = []
    stack_sum = None
    for level in range(4):
        layer_vals = depth_stack[level].astype(F32)
        term = dwa_weights[level] * layer_vals
        stack_sum = term if stack_sum is None else stack_sum + term
        partial_dots.append(jnp.sum(layer_vals * grad_out))
    grad_stack = dwa_weights[:4, None, None] * grad_out[None]
    grad_block = dwa_weights[4] * grad_out
    grad_down_in = grad_block.astype(BF)

    qkv, normed = project(tokens, gain_one, bias_one, proj_qkv, cos, sin)
    heads_in, lse = attend(qkv, prefix_len)
    resid = inputs_f + jnp.dot(heads_in, proj_out, preferred_element_type=F32)
    normed_two = layer_norm(resid, gain_two, bias_two).astype(BF)
    before = jnp.dot(normed_two, proj_up, preferred_element_type=F32) + bias_up
    hidden = jax.nn.gelu(before, approximate=True).astype(BF)
    block_out = resid + jnp.dot(hidden, proj_down, preferred_element_type=F32) + bias_down
    result = dwa_weights[4] * block_out + stack_sum
    partial_dots.append(jnp.sum(block_out * grad_out))
    grad_dwa = sum_everywhere(jnp.stack(partial_dots), count)

    grad_w_down = tn(hidden, grad_down_in).astype(BF)
    own_down = scatter_grad([grad_w_down], count, owners)
    grad_b_down = jnp.sum(grad_down_in.astype(F32), axis=0)
    grad_hidden = nt(grad_down_in, proj_down)
    gelu_pull = jax.vjp(partial(jax.nn.gelu, approximate=True), before)[1]
    grad_before = gelu_pull(grad_hidden)[0].astype(BF)
    grad_w_up = tn(normed_two, grad_before).astype(BF)
    own_up = scatter_grad([grad_w_up], count, owners)
    grad_b_up = jnp.sum(grad_before.astype(F32), axis=0)
    grad_normed_two = nt(grad_before, proj_up)
    second_pull = jax.vjp(layer_norm, resid, gain_two, bias_two)[1]
    grad_resid_norm, grad_gain_two, grad_bias_two = second_pull(grad_normed_two)
    grad_resid = grad_block + grad_resid_norm
    grad_attn = grad_resid.astype(BF)
    grad_w_out = tn(heads_in, grad_attn).astype(BF)
    own_out = scatter_grad([grad_w_out], count, owners)
    grad_heads = nt(grad_attn, proj_out).astype(BF)
    own_gain_two, own_bias_two, own_b_down, own_b_up = scatter_vectors(
        (grad_gain_two, grad_bias_two, grad_b_down, grad_b_up), count, owners
    )

    grads = attend_back(qkv, grad_heads, lse, cos, sin, prefix_len)
    own_qkv = scatter_grad([tn(normed, g).astype(BF) for g in grads], count, owners)
    grad_normed = None
    for k, g in enumerate(grads):
        term = nt(g, proj_qkv[:, k * model_width : (k + 1) * model_width])
        grad_normed = term if grad_normed is None else grad_normed + term
    first_pull = jax.vjp(layer_norm, inputs_f, gain_one, bias_one)[1]
    grad_input_norm, grad_gain_one, grad_bias_one = first_pull(grad_normed)
    grad_tokens = grad_resid + grad_input_norm
    own_gain_one, own_bias_one = scatter_vectors((grad_gain_one, grad_bias_one), count, owners)
    return (
        result.astype(BF),
        grad_tokens,
        grad_stack,
        own_gain_one,
        own_bias_one,
        own_qkv,
        own_out,
        own_gain_two,
        own_bias_two,
        own_up,
        own_b_up,
        own_down,
        own_b_down,
        grad_dwa,
    )


def solution(mesh):
    row = P("fsdp", None)
    vec = P("fsdp")
    stack = P(None, "fsdp", None)
    return jax.shard_map(
        partial(shards, mesh.shape["fsdp"]),
        mesh=mesh,
        in_specs=(row, stack, P(), vec, vec, row, row, vec, vec, row, vec, row, vec, P(), row),
        out_specs=(row, row, stack, vec, vec, row, row, vec, vec, row, vec, row, vec, P()),
        check_vma=False,
    )
```
